128 devices in a mesh: shard: 32 (over y, x, core), tile: 4 (over z).
Axes of the slice: x: 4, y: 4, z: 4, core: 2. Of those that a mesh axis runs over, the one named last changes fastest.
Arguments:
- embeddings: float32 [131072, 768], P(('shard', 'tile')), may hold values from -12 to 12
- cluster_ids: int32 [131072], P(('shard', 'tile')), may hold values from 0 to 511, as said below
Outputs:
- soft_max_sim: float32 [131072], P(('shard', 'tile'))
The draws below stay inside these ranges and needn't reach their ends.
Inputs may be any that keep to these rules, and one draw needn't show every extreme that they name: `cluster_ids`: cluster c is owned by group c // 16. Each device holds at most 64 rows of one group's clusters; in every draw, for each tile index, some group gets exactly 64 rows from every device of that tile index.
All inputs are finite; a program needn't handle non-finite values.
Results may differ from the reference program's by a relative error of at most 0.00053.
Values may be sent and summed in bfloat16 or wider, within the bound.
A program may use at most 64 MiB of HBM per device.

```python
import math
import jax
import jax.numpy as jnp
from jax import lax

D = 768
ROW_DEV = 1024
KG = 16
CAP = 64
N_SHARD = 32
N_TILE = 4


def cluster_draw(key):
    devices = N_SHARD * N_TILE
    base_key = jax.random.fold_in(key, 11)
    first_key, second_key, third_key, fourth_key = jax.random.split(base_key, 4)
    full_owner = jax.random.randint(first_key, (N_TILE,), 0, N_SHARD)
    device_full = jnp.tile(full_owner, N_SHARD)
    slot_total = N_SHARD * CAP
    shuffled = jax.vmap(lambda single: jax.random.permutation(single, slot_total))(jax.random.split(second_key, devices))
    slot_owner = shuffled // CAP
    is_full = (slot_owner == device_full[:, None]).astype(jnp.int32)
    arranged = jnp.argsort(is_full, axis=1, stable=True)
    others = jnp.take_along_axis(slot_owner, arranged, axis=1)[:, :ROW_DEV - CAP]
    owners = jnp.concatenate([jnp.broadcast_to(device_full[:, None], (devices, CAP)), others], axis=1)
    mixing = jax.vmap(lambda single: jax.random.permutation(single, ROW_DEV))(jax.random.split(third_key, devices))
    owners = jnp.take_along_axis(owners, mixing, axis=1)
    local = jax.random.randint(fourth_key, (devices, ROW_DEV), 0, KG)
    return (owners * KG + local).reshape(devices * ROW_DEV).astype(jnp.int32)


def draw_cluster_ids(key, part):
    return cluster_draw(key)


def draw_embeddings(key, part):
    labels = cluster_draw(key)
    total = labels.shape[0]
    own_key = jax.random.fold_in(key, 23)
    coin_key = jax.random.fold_in(own_key, 0)
    base_key = jax.random.fold_in(own_key, 1)
    noise_key = jax.random.fold_in(own_key, 4)
    relative_key = jax.random.fold_in(own_key, 5)
    stretch_key = jax.random.fold_in(own_key, 6)
    order = jnp.argsort(labels, stable=True).astype(jnp.int32)
    position = jnp.arange(total, dtype=jnp.int32)
    sorted_labels = labels[order]
    previous_same = jnp.concatenate([jnp.zeros((1,), bool), sorted_labels[1:] == sorted_labels[:-1]])
    coin = jax.random.randint(coin_key, (total,), 0, 4) == 0
    copy_sorted = previous_same & (position % 2 == 1) & coin
    predecessor = order[jnp.maximum(position - 1, 0)]
    source_sorted = jnp.where(copy_sorted, predecessor, order)
    is_copy = jnp.zeros((total,), bool).at[order].set(copy_sorted)
    source = jnp.zeros((total,), jnp.int32).at[order].set(source_sorted)
    base = jax.random.truncated_normal(base_key, -6.0, 6.0, (total, D), jnp.float32)
    noise = jax.random.normal(noise_key, (total, D), jnp.float32)
    relative = jnp.exp(jax.random.uniform(relative_key, (total, 1), jnp.float32, math.log(0.03), math.log(0.5)))
    stretch = jnp.exp(jax.random.uniform(stretch_key, (total, 1), jnp.float32, math.log(0.5), math.log(2.0)))
    copied = stretch * (base[source] + relative * noise)
    result = jnp.where(is_copy[:, None], copied, base)
    return jnp.clip(result, -12.0, 12.0).astype(jnp.float32)


def setup_inputs(seed: int = 0) -> dict:
    key_list = jax.random.split(jax.random.key(seed), 3)
    embeddings = draw_embeddings(jax.random.fold_in(key_list[2], 71), 0)
    cluster_ids = draw_cluster_ids(jax.random.fold_in(key_list[2], 71), 0)
    return {"embeddings": embeddings, "cluster_ids": cluster_ids}


sharpness = 30.0
epsilon = 1e-06

def unit_rows(embeddings):
    energy = lax.optimization_barrier(jnp.sum(embeddings * embeddings, axis=1, keepdims=True))
    return (embeddings * lax.rsqrt(energy + epsilon)).astype(jnp.bfloat16)

def reference(embeddings, cluster_ids):
    unit = unit_rows(embeddings).astype(jnp.float32)
    total_rows = unit.shape[0]
    owner = cluster_ids // KG
    group_slots = 2 * ROW_DEV * N_TILE
    order = jnp.argsort(owner, stable=True).astype(jnp.int32)
    counts = lax.optimization_barrier(jnp.sum((owner[:, None] == jnp.arange(N_SHARD, dtype=jnp.int32)[None, :]).astype(jnp.int32), axis=0))
    starts = (jnp.cumsum(counts) - counts).astype(jnp.int32)
    block = min(1024, group_slots)

    def one_group(group):
        place = jnp.arange(group_slots, dtype=jnp.int32)
        valid = place < counts[group]
        members = order[jnp.where(valid, starts[group] + place, 0)]
        labels = jnp.where(valid, cluster_ids[members], -1)
        vectors = unit[members]

        def left_block(index):
            lower = (index * block).astype(jnp.int32)
            rows_block = lax.dynamic_slice_in_dim(vectors, lower, block)
            labels_block = lax.dynamic_slice_in_dim(labels, lower, block)
            place_block = lower + jnp.arange(block, dtype=jnp.int32)
            scores = jnp.dot(rows_block, vectors.T, preferred_element_type=jnp.float32, precision=lax.Precision.HIGHEST)
            same = (labels_block[:, None] == labels[None, :]) & (labels_block[:, None] >= 0)
            same = same & (place_block[:, None] != place[None, :])
            return lax.optimization_barrier(jnp.sum(jnp.where(same, jnp.exp(sharpness * scores), 0.0), axis=1))
        totals = lax.map(left_block, jnp.arange(group_slots // block, dtype=jnp.int32)).reshape(group_slots)
        targets = jnp.where(valid, members, total_rows)
        return (totals, targets)
    totals, targets = lax.map(one_group, jnp.arange(N_SHARD, dtype=jnp.int32))
    placed = jnp.zeros((total_rows,), jnp.float32).at[targets.reshape(-1)].set(totals.reshape(-1), mode='drop')
    return jnp.log(1.0 + placed)
```

```python
import functools
import math

import jax
import jax.numpy as jnp
from jax import lax
from jax.experimental import pallas as pl
from jax.experimental.pallas import tpu as pltpu
from jax.sharding import PartitionSpec as P

KG = 16
SHARDS = 32
CAP = 64
SLOTS = SHARDS * CAP
LANES = 128
MESH = pl.DeviceIdType.MESH

sharpness = 30.0
epsilon = 1e-06
EXP2_SCALE = sharpness / math.log(2.0)
ROW_BLOCK = 512


def unit_rows(embeddings):
    energy = jnp.sum(embeddings * embeddings, axis=1, keepdims=True)
    return (embeddings * lax.rsqrt(energy + epsilon)).astype(jnp.bfloat16)


def kernel(
    rows_ref, labels_ref, out_ref,
    rows, labels, row_labels, row_acc, col_f, col_h, col_in, totals, returned,
    local_sem, a2a_send, a2a_recv, lab_send, lab_recv, z_send, z_recv,
    zlab_send, zlab_recv, col_send, col_recv, ret_send, ret_recv,
):
    s = lax.axis_index("shard")
    t = lax.axis_index("tile")
    core = s % 2
    x = (s // 2) % 4
    y = s // 8
    up = (t + 1) % 4
    down = (t + 3) % 4
    high = t // 2
    f_device = (t + 2) * (1 - high) + (3 - t) * high
    h_device = t + 1 - 2 * (t % 2)
    f_slot = 2 - t % 2
    h_slot = 1 + t % 2

    def chip_at(step, sign):
        q = (step * 5) % 16
        return ((y + sign * (q // 4) + 4) % 4) * 4 + (x + sign * (q % 4) + 4) % 4

    def peer(i, sign):
        return chip_at(i // 2, sign) * 2 + (core + i % 2) % 2

    def chunk(slot, p):
        return rows.at[slot, pl.ds(pl.multiple_of(p * CAP, CAP), CAP)]

    barrier = pltpu.get_barrier_semaphore()

    @pl.loop(1, SHARDS)
    def _(i):
        pl.semaphore_signal(barrier, inc=1, device_id=(peer(i, 1), t), device_id_type=MESH)

    @pl.loop(1, 4)
    def _(i):
        pl.semaphore_signal(barrier, inc=1, device_id=(s, (t + i) % 4), device_id_type=MESH)

    own_rows = pltpu.make_async_copy(rows_ref.at[s], chunk(0, s), local_sem.at[0])
    own_labels = pltpu.make_async_copy(labels_ref.at[s], labels.at[0, s], local_sem.at[1])
    own_rows.start()
    own_labels.start()
    pl.semaphore_wait(barrier, SHARDS - 1 + 3)

    def label_copy(i):
        p = peer(i, 1)
        return pltpu.make_async_remote_copy(
            src_ref=labels_ref.at[p], dst_ref=labels.at[0, s],
            send_sem=lab_send.at[i], recv_sem=lab_recv.at[i],
            device_id=(p, t), device_id_type=MESH,
        )

    def label_arrival(i):
        p = peer(i, -1)
        return pltpu.make_async_remote_copy(
            src_ref=labels_ref.at[p], dst_ref=labels.at[0, p],
            send_sem=lab_send.at[i], recv_sem=lab_recv.at[i],
            device_id=(p, t), device_id_type=MESH,
        )

    def row_copy(i):
        p = peer(i, 1)
        return pltpu.make_async_remote_copy(
            src_ref=rows_ref.at[p], dst_ref=chunk(0, s),
            send_sem=a2a_send.at[i], recv_sem=a2a_recv.at[i],
            device_id=(p, t), device_id_type=MESH,
        )

    def row_arrival(i):
        p = peer(i, -1)
        return pltpu.make_async_remote_copy(
            src_ref=rows_ref.at[p], dst_ref=chunk(0, p),
            send_sem=a2a_send.at[i], recv_sem=a2a_recv.at[i],
            device_id=(p, t), device_id_type=MESH,
        )

    def z_copy(source, target, device, i):
        p = peer(i, -1)
        return pltpu.make_async_remote_copy(
            src_ref=chunk(source, p), dst_ref=chunk(target, p),
            send_sem=z_send.at[target - 1, i], recv_sem=z_recv.at[target - 1, i],
            device_id=(s, device), device_id_type=MESH,
        )

    def zlab_copy(source, target, device):
        return pltpu.make_async_remote_copy(
            src_ref=labels.at[source], dst_ref=labels.at[target],
            send_sem=zlab_send.at[target - 1], recv_sem=zlab_recv.at[target - 1],
            device_id=(s, device), device_id_type=MESH,
        )

    @pl.loop(1, SHARDS)
    def _(i):
        label_copy(i).start()

    @pl.loop(1, SHARDS)
    def _(i):
        row_copy(i).start()

    def send_own(i):
        @pl.when(t != 3)
        def _():
            z_copy(0, 2, up, i).start()

        @pl.when(t != 2)
        def _():
            z_copy(0, 1, down, i).start()

    def relay(i):
        @pl.when(t == 3)
        def _():
            z_copy(0, 2, up, i).wait_recv()
            z_copy(2, 2, up, i).start()

        @pl.when(t == 2)
        def _():
            z_copy(0, 1, down, i).wait_recv()
            z_copy(1, 1, down, i).start()

    own_rows.wait()
    own_labels.wait()
    send_own(0)

    def forward(i):
        row_arrival(i).wait_recv()
        send_own(i)

        @pl.when(i % 2 == 1)
        def _():
            relay(i // 2)

    @pl.loop(1, 6)
    def _(i):
        forward(i)

    @pl.loop(1, SHARDS)
    def _(i):
        label_arrival(i).wait_recv()

    @pl.when(t != 3)
    def _():
        zlab_copy(0, 2, up).start()

    @pl.when(t != 2)
    def _():
        zlab_copy(0, 1, down).start()

    def pair_labels(slot, c):
        return labels[slot, 2 * c] + labels[slot, 2 * c + 1]

    @pl.loop(0, SLOTS // LANES)
    def _(c):
        wide = jnp.broadcast_to(pair_labels(0, c), (LANES, LANES))
        row_labels[pl.ds(pl.multiple_of(c * LANES, LANES), LANES), :] = wide.astype(jnp.float32).T
        row_acc[pl.ds(pl.multiple_of(c * LANES, LANES), LANES), :] = jnp.zeros((LANES, LANES), jnp.float32)

    @pl.loop(6, SHARDS)
    def _(i):
        forward(i)

    zlab_copy(0, 2, up).wait_recv()
    zlab_copy(0, 1, down).wait_recv()

    @pl.when(t == 3)
    def _():
        zlab_copy(2, 2, up).start()

    @pl.when(t == 2)
    def _():
        zlab_copy(1, 1, down).start()

    def square(slot, chips, row_start, row_blocks, col_ref):
        columns = jnp.concatenate(
            [rows[slot, pl.ds(pl.multiple_of(c * LANES, LANES), LANES), :] for c in chips], axis=0
        )
        column_labels = [
            jnp.broadcast_to(pair_labels(slot, c), (8, LANES)).astype(jnp.float32)[0:1] for c in chips
        ]

        def block(m, sums):
            start = pl.multiple_of(row_start + m * ROW_BLOCK, ROW_BLOCK)
            here = pl.ds(start, ROW_BLOCK)
            scores = lax.dot_general(
                rows[0, here, :], columns, (((1,), (1,)), ((), ())),
                preferred_element_type=jnp.float32,
            )
            left = row_labels[here, :]
            added = None
            new_sums = []
            for n, c in enumerate(chips):
                same = left == column_labels[n]
                if col_ref is None:
                    down_index = lax.broadcasted_iota(jnp.int32, (ROW_BLOCK, LANES), 0)
                    along = lax.broadcasted_iota(jnp.int32, (ROW_BLOCK, LANES), 1)
                    same = same & ((down_index - along) != (c * LANES - start))
                terms = jnp.where(
                    same, jnp.exp2(scores[:, n * LANES:(n + 1) * LANES] * EXP2_SCALE), 0.0
                )
                added = terms if added is None else added + terms
                if col_ref is not None:
                    new_sums.append(sums[n] + jnp.sum(terms, axis=0, keepdims=True))
            row_acc[here, :] += added
            return tuple(new_sums)

        zero = tuple(jnp.zeros((1, LANES), jnp.float32) for _ in chips) if col_ref is not None else ()
        sums = lax.fori_loop(0, row_blocks, block, zero)
        if col_ref is not None:
            for n, c in enumerate(chips):
                col_ref[c] = sums[n]

    @pl.loop(0, 8)
    def _(j):
        @pl.loop(0, 2)
        def _(k):
            relay(16 + 2 * j + k)

        chips = [chip_at(2 * j, -1), chip_at(2 * j + 1, -1)]
        square(0, chips, 0, SLOTS // ROW_BLOCK, None)

        @pl.loop(0, 4)
        def _(k):
            z_copy(0, f_slot, up, 4 * j + k).wait_recv()

            @pl.when(t < 2)
            def _():
                z_copy(0, h_slot, up, 4 * j + k).wait_recv()

        square(f_slot, chips, 0, SLOTS // ROW_BLOCK, col_f)
        for n in range(2):
            half = (chips[n] // 8 + t) % 2
            square(h_slot, [chips[n]], half * (SLOTS // 2), SLOTS // 2 // ROW_BLOCK, col_h)

    def col_copy(source, k, device):
        return pltpu.make_async_remote_copy(
            src_ref=source, dst_ref=col_in.at[k],
            send_sem=col_send.at[k], recv_sem=col_recv.at[k],
            device_id=(s, device), device_id_type=MESH,
        )

    copy_f = col_copy(col_f, 0, f_device)
    copy_h = col_copy(col_h, 1, h_device)
    copy_f.start()
    copy_h.start()

    @pl.loop(0, SLOTS // LANES)
    def _(c):
        part = row_acc[pl.ds(pl.multiple_of(c * LANES, LANES), LANES), :]
        totals[c] = jnp.sum(part.T, axis=0, keepdims=True)

    copy_f.wait_recv()
    copy_h.wait_recv()

    @pl.loop(0, SLOTS // LANES)
    def _(c):
        totals[c] = totals[c] + col_in[0, c] + col_in[1, c]

    def ret_copy(i, p, place):
        return pltpu.make_async_remote_copy(
            src_ref=totals.at[p // 2], dst_ref=returned.at[place],
            send_sem=ret_send.at[i], recv_sem=ret_recv.at[i],
            device_id=(p, t), device_id_type=MESH,
        )

    @pl.loop(1, SHARDS)
    def _(i):
        ret_copy(i, peer(i, 1), s).start()

    returned[s] = totals[s // 2]

    @pl.loop(1, SHARDS)
    def _(i):
        label_copy(i).wait_send()
        row_copy(i).wait_send()

    @pl.loop(0, SHARDS)
    def _(i):
        z_copy(0, 1, down, i).wait_send()
        z_copy(0, 2, up, i).wait_send()

    zlab_copy(0, 1, down).wait_send()
    zlab_copy(0, 2, up).wait_send()
    copy_f.wait_send()
    copy_h.wait_send()

    @pl.loop(1, SHARDS)
    def _(i):
        p = peer(i, -1)
        ret_copy(i, p, p).wait_recv()
        ret_copy(i, peer(i, 1), s).wait_send()

    out_ref[...] = returned[...]


def exchange(outgoing, outgoing_labels):
    width = outgoing.shape[-1]
    dma = pltpu.SemaphoreType.DMA
    return pl.pallas_call(
        kernel,
        out_shape=jax.ShapeDtypeStruct((SHARDS, 1, LANES), jnp.float32),
        in_specs=[pl.BlockSpec(memory_space=pl.ANY), pl.BlockSpec(memory_space=pltpu.VMEM)],
        out_specs=pl.BlockSpec(memory_space=pltpu.VMEM),
        scratch_shapes=[
            pltpu.VMEM((3, SLOTS, width), jnp.bfloat16),
            pltpu.VMEM((3, SHARDS, 1, LANES), jnp.int32),
            pltpu.VMEM((SLOTS, LANES), jnp.float32),
            pltpu.VMEM((SLOTS, LANES), jnp.float32),
            pltpu.VMEM((SLOTS // LANES, 1, LANES), jnp.float32),
            pltpu.VMEM((SLOTS // LANES, 1, LANES), jnp.float32),
            pltpu.VMEM((2, SLOTS // LANES, 1, LANES), jnp.float32),
            pltpu.VMEM((SLOTS // LANES, 1, LANES), jnp.float32),
            pltpu.VMEM((SHARDS, 1, LANES), jnp.float32),
            dma((2,)), dma((SHARDS,)), dma((SHARDS,)), dma((SHARDS,)), dma((SHARDS,)),
            dma((2, SHARDS)), dma((2, SHARDS)), dma((2,)), dma((2,)), dma((2,)), dma((2,)),
            dma((SHARDS,)), dma((SHARDS,)),
        ],
        compiler_params=pltpu.CompilerParams(collective_id=0, has_side_effects=True),
    )(outgoing, outgoing_labels)


def body(embeddings, cluster_ids):
    unit = unit_rows(embeddings)
    owner = cluster_ids // KG
    onehot = (owner[:, None] == jnp.arange(SHARDS, dtype=jnp.int32)[None, :]).astype(jnp.int32)
    ranks = jnp.sum((jnp.cumsum(onehot, axis=0) - 1) * onehot, axis=1)
    slots = owner * CAP + ranks
    outgoing = jnp.zeros((SLOTS, unit.shape[1]), jnp.bfloat16).at[slots].set(unit)
    core = lax.axis_index("shard") % 2
    outgoing_labels = jnp.full((SLOTS,), -1, jnp.int32).at[slots].set(cluster_ids)
    outgoing_labels = outgoing_labels.reshape(SHARDS, 1, CAP)
    blank = jnp.zeros_like(outgoing_labels)
    outgoing_labels = jnp.where(
        core == 0,
        jnp.concatenate([outgoing_labels, blank], axis=2),
        jnp.concatenate([blank, outgoing_labels], axis=2),
    )
    returned = exchange(outgoing.reshape(SHARDS, CAP, unit.shape[1]), outgoing_labels)
    totals = returned.reshape(SHARDS * LANES)[owner * LANES + core * CAP + ranks]
    return jnp.log(1.0 + totals)


def solution(mesh):
    in_specs = (P(("shard", "tile"), None), P(("shard", "tile")))
    out_specs = P(("shard", "tile"))
    return jax.shard_map(body, mesh=mesh, in_specs=in_specs, out_specs=out_specs, check_vma=False)
```

```python
import math

import jax
import jax.numpy as jnp
from jax import lax
from jax.experimental import pallas as pl
from jax.experimental.pallas import tpu as pltpu
from jax.sharding import PartitionSpec as P

KG = 16
SHARDS = 32
CAP = 64
SLOTS = SHARDS * CAP
LANES = 128
MESH = pl.DeviceIdType.MESH

sharpness = 30.0
epsilon = 1e-06
EXP2_SCALE = sharpness / math.log(2.0)
ROW_BLOCK = 512
PLACE = 512


def kernel(
    data_ref, ids_ref, out_ref,
    unit, rows_ref, labels_ref, rows, labels, row_labels, row_acc, col_f, col_h, col_in, totals, returned,
    local_sem, a2a_send, a2a_recv, lab_send, lab_recv, z_send, z_recv,
    zlab_send, zlab_recv, col_send, col_recv, ret_send, ret_recv,
):
    s = lax.axis_index("shard")
    t = lax.axis_index("tile")
    core = s % 2
    x = (s // 2) % 4
    y = s // 8
    up = (t + 1) % 4
    down = (t + 3) % 4
    high = t // 2
    f_device = (t + 2) * (1 - high) + (3 - t) * high
    h_device = t + 1 - 2 * (t % 2)
    f_slot = 2 - t % 2
    h_slot = 1 + t % 2

    def chip_at(step, sign):
        q = (step * 5) % 16
        return ((y + sign * (q // 4) + 4) % 4) * 4 + (x + sign * (q % 4) + 4) % 4

    def peer(i, sign):
        return chip_at(i // 2, sign) * 2 + (core + i % 2) % 2

    def chunk(slot, p):
        return rows.at[slot, pl.ds(pl.multiple_of(p * CAP, CAP), CAP)]

    barrier = pltpu.get_barrier_semaphore()

    @pl.loop(1, SHARDS)
    def _(i):
        pl.semaphore_signal(barrier, inc=1, device_id=(peer(i, 1), t), device_id_type=MESH)

    @pl.loop(1, 4)
    def _(i):
        pl.semaphore_signal(barrier, inc=1, device_id=(s, (t + i) % 4), device_id_type=MESH)

    ids = ids_ref[...]
    owner = lax.shift_right_logical(ids, 4)
    local = lax.bitwise_and(ids, KG - 1)
    count = ids.shape[1]
    is_owner = lax.broadcasted_iota(jnp.int32, (SHARDS, count), 0) == owner
    onehot = jnp.where(is_owner, 1.0, 0.0)
    onehot_bf16 = onehot.astype(jnp.bfloat16)
    earlier = lax.broadcasted_iota(jnp.int32, (count, count), 0) < lax.broadcasted_iota(
        jnp.int32, (count, count), 1
    )
    before = lax.dot_general(
        onehot_bf16, jnp.where(earlier, 1.0, 0.0).astype(jnp.bfloat16), (((1,), (0,)), ((), ())),
        preferred_element_type=jnp.float32,
    )
    ranks = jnp.sum(before * onehot, axis=0, keepdims=True).astype(jnp.int32)
    slots = owner * CAP + ranks

    @pl.loop(0, count // LANES)
    def _(k):
        here = pl.ds(pl.multiple_of(k * LANES, LANES), LANES)
        block = data_ref[here, :]
        energy = jnp.sum(block * block, axis=1, keepdims=True)
        unit[here, :] = (block * lax.rsqrt(energy + epsilon)).astype(jnp.bfloat16)

    tags = jnp.broadcast_to((local + 1).astype(jnp.float32), (8, count)).astype(jnp.bfloat16)
    lane = lax.broadcasted_iota(jnp.int32, (1, LANES), 1)
    in_half = (lane // CAP) == core

    def place(k):
        slot = lax.broadcasted_iota(jnp.int32, (PLACE, count), 0) + k * PLACE
        chosen = jnp.where(slot == slots, 1.0, 0.0).astype(jnp.bfloat16)
        rows_out = lax.dot_general(
            chosen, unit[...], (((1,), (0,)), ((), ())), preferred_element_type=jnp.float32
        ).astype(jnp.bfloat16)
        for m in range(PLACE // CAP):
            rows_ref[k * (PLACE // CAP) + m] = rows_out[m * CAP:(m + 1) * CAP]
        tags_out = lax.dot_general(
            tags, chosen, (((1,), (1,)), ((), ())), preferred_element_type=jnp.float32
        )
        for m in range(PLACE // LANES):
            both = tags_out[:, m * LANES:(m + 1) * LANES]
            swapped = pltpu.roll(both, CAP, 1)
            for b in range(2):
                value = jnp.where(core == b, both, swapped)[0:1]
                labels_ref[k * (PLACE // CAP) + 2 * m + b] = jnp.where(in_half, value, 0.0)

    @pl.loop(0, SLOTS // PLACE)
    def _(k):
        place(k)

    own_rows = pltpu.make_async_copy(rows_ref.at[s], chunk(0, s), local_sem.at[0])
    own_labels = pltpu.make_async_copy(labels_ref.at[s], labels.at[0, s], local_sem.at[1])
    own_rows.start()
    own_labels.start()
    pl.semaphore_wait(barrier, SHARDS - 1 + 3)

    def label_copy(i):
        p = peer(i, 1)
        return pltpu.make_async_remote_copy(
            src_ref=labels_ref.at[p], dst_ref=labels.at[0, s],
            send_sem=lab_send.at[i], recv_sem=lab_recv.at[i],
            device_id=(p, t), device_id_type=MESH,
        )

    def label_arrival(i):
        p = peer(i, -1)
        return pltpu.make_async_remote_copy(
            src_ref=labels_ref.at[p], dst_ref=labels.at[0, p],
            send_sem=lab_send.at[i], recv_sem=lab_recv.at[i],
            device_id=(p, t), device_id_type=MESH,
        )

    def row_copy(i):
        p = peer(i, 1)
        return pltpu.make_async_remote_copy(
            src_ref=rows_ref.at[p], dst_ref=chunk(0, s),
            send_sem=a2a_send.at[i], recv_sem=a2a_recv.at[i],
            device_id=(p, t), device_id_type=MESH,
        )

    def row_arrival(i):
        p = peer(i, -1)
        return pltpu.make_async_remote_copy(
            src_ref=rows_ref.at[p], dst_ref=chunk(0, p),
            send_sem=a2a_send.at[i], recv_sem=a2a_recv.at[i],
            device_id=(p, t), device_id_type=MESH,
        )

    def z_copy(source, target, device, i):
        p = peer(i, -1)
        return pltpu.make_async_remote_copy(
            src_ref=chunk(source, p), dst_ref=chunk(target, p),
            send_sem=z_send.at[target - 1, i], recv_sem=z_recv.at[target - 1, i],
            device_id=(s, device), device_id_type=MESH,
        )

    def zlab_copy(source, target, device):
        return pltpu.make_async_remote_copy(
            src_ref=labels.at[source], dst_ref=labels.at[target],
            send_sem=zlab_send.at[target - 1], recv_sem=zlab_recv.at[target - 1],
            device_id=(s, device), device_id_type=MESH,
        )

    @pl.loop(1, SHARDS)
    def _(i):
        label_copy(i).start()

    @pl.loop(1, SHARDS)
    def _(i):
        row_copy(i).start()

    def send_own(i):
        @pl.when(t != 3)
        def _():
            z_copy(0, 2, up, i).start()

        @pl.when(t != 2)
        def _():
            z_copy(0, 1, down, i).start()

    def relay(i):
        @pl.when(t == 3)
        def _():
            z_copy(0, 2, up, i).wait_recv()
            z_copy(2, 2, up, i).start()

        @pl.when(t == 2)
        def _():
            z_copy(0, 1, down, i).wait_recv()
            z_copy(1, 1, down, i).start()

    own_rows.wait()
    own_labels.wait()
    send_own(0)

    def forward(i):
        row_arrival(i).wait_recv()
        send_own(i)

        @pl.when(i % 2 == 1)
        def _():
            relay(i // 2)

    @pl.loop(1, 6)
    def _(i):
        forward(i)

    @pl.loop(1, SHARDS)
    def _(i):
        label_arrival(i).wait_recv()

    @pl.when(t != 3)
    def _():
        zlab_copy(0, 2, up).start()

    @pl.when(t != 2)
    def _():
        zlab_copy(0, 1, down).start()

    def pair_labels(slot, c):
        return labels[slot, 2 * c] + labels[slot, 2 * c + 1]

    @pl.loop(0, SLOTS // LANES)
    def _(c):
        wide = jnp.broadcast_to(pair_labels(0, c), (LANES, LANES))
        row_labels[pl.ds(pl.multiple_of(c * LANES, LANES), LANES), :] = wide.T
        row_acc[pl.ds(pl.multiple_of(c * LANES, LANES), LANES), :] = jnp.zeros((LANES, LANES), jnp.float32)

    @pl.loop(6, SHARDS)
    def _(i):
        forward(i)

    zlab_copy(0, 2, up).wait_recv()
    zlab_copy(0, 1, down).wait_recv()

    @pl.when(t == 3)
    def _():
        zlab_copy(2, 2, up).start()

    @pl.when(t == 2)
    def _():
        zlab_copy(1, 1, down).start()

    def square(slot, chips, row_start, row_blocks, col_ref):
        columns = jnp.concatenate(
            [rows[slot, pl.ds(pl.multiple_of(c * LANES, LANES), LANES), :] for c in chips], axis=0
        )
        column_labels = [
            pair_labels(slot, c) for c in chips
        ]

        def block(m, sums):
            start = pl.multiple_of(row_start + m * ROW_BLOCK, ROW_BLOCK)
            here = pl.ds(start, ROW_BLOCK)
            scores = lax.dot_general(
                rows[0, here, :], columns, (((1,), (1,)), ((), ())),
                preferred_element_type=jnp.float32,
            )
            left = row_labels[here, :]
            added = None
            new_sums = []
            for n, c in enumerate(chips):
                same = left == column_labels[n]
                if col_ref is None:
                    down_index = lax.broadcasted_iota(jnp.int32, (ROW_BLOCK, LANES), 0)
                    along = lax.broadcasted_iota(jnp.int32, (ROW_BLOCK, LANES), 1)
                    same = same & ((down_index - along) != (c * LANES - start))
                terms = jnp.where(
                    same, jnp.exp2(scores[:, n * LANES:(n + 1) * LANES] * EXP2_SCALE), 0.0
                )
                added = terms if added is None else added + terms
                if col_ref is not None:
                    new_sums.append(sums[n] + jnp.sum(terms, axis=0, keepdims=True))
            row_acc[here, :] += added
            return tuple(new_sums)

        zero = tuple(jnp.zeros((1, LANES), jnp.float32) for _ in chips) if col_ref is not None else ()
        sums = lax.fori_loop(0, row_blocks, block, zero)
        if col_ref is not None:
            for n, c in enumerate(chips):
                col_ref[c] = sums[n]

    @pl.loop(0, 8)
    def _(j):
        @pl.loop(0, 2)
        def _(k):
            relay(16 + 2 * j + k)

        chips = [chip_at(2 * j, -1), chip_at(2 * j + 1, -1)]
        square(0, chips, 0, SLOTS // ROW_BLOCK, None)

        @pl.loop(0, 4)
        def _(k):
            z_copy(0, f_slot, up, 4 * j + k).wait_recv()

            @pl.when(t < 2)
            def _():
                z_copy(0, h_slot, up, 4 * j + k).wait_recv()

        square(f_slot, chips, 0, SLOTS // ROW_BLOCK, col_f)
        for n in range(2):
            half = (chips[n] // 8 + t) % 2
            square(h_slot, [chips[n]], half * (SLOTS // 2), SLOTS // 2 // ROW_BLOCK, col_h)

    def col_copy(source, k, device):
        return pltpu.make_async_remote_copy(
            src_ref=source, dst_ref=col_in.at[k],
            send_sem=col_send.at[k], recv_sem=col_recv.at[k],
            device_id=(s, device), device_id_type=MESH,
        )

    copy_f = col_copy(col_f, 0, f_device)
    copy_h = col_copy(col_h, 1, h_device)
    copy_f.start()
    copy_h.start()

    @pl.loop(0, SLOTS // LANES)
    def _(c):
        part = row_acc[pl.ds(pl.multiple_of(c * LANES, LANES), LANES), :]
        totals[c] = jnp.sum(part.T, axis=0, keepdims=True)

    copy_f.wait_recv()
    copy_h.wait_recv()

    @pl.loop(0, SLOTS // LANES)
    def _(c):
        totals[c] = totals[c] + col_in[0, c] + col_in[1, c]

    def ret_copy(i, p, place):
        return pltpu.make_async_remote_copy(
            src_ref=totals.at[p // 2], dst_ref=returned.at[place],
            send_sem=ret_send.at[i], recv_sem=ret_recv.at[i],
            device_id=(p, t), device_id_type=MESH,
        )

    @pl.loop(1, SHARDS)
    def _(i):
        ret_copy(i, peer(i, 1), s).start()

    returned[s] = totals[s // 2]

    @pl.loop(1, SHARDS)
    def _(i):
        label_copy(i).wait_send()
        row_copy(i).wait_send()

    @pl.loop(0, SHARDS)
    def _(i):
        z_copy(0, 1, down, i).wait_send()
        z_copy(0, 2, up, i).wait_send()

    zlab_copy(0, 1, down).wait_send()
    zlab_copy(0, 2, up).wait_send()
    copy_f.wait_send()
    copy_h.wait_send()

    @pl.loop(1, SHARDS)
    def _(i):
        p = peer(i, -1)
        ret_copy(i, p, p).wait_recv()
        ret_copy(i, peer(i, 1), s).wait_send()

    back = returned[:, 0, :]
    picked = None
    for _ in range(3):
        piece = back.astype(jnp.bfloat16)
        back = back - piece.astype(jnp.float32)
        part = lax.dot_general(
            piece, onehot_bf16, (((0,), (0,)), ((), ())), preferred_element_type=jnp.float32
        )
        picked = part if picked is None else picked + part
    at_rank = lax.broadcasted_iota(jnp.int32, (LANES, count), 0) == core * CAP + ranks
    total = jnp.sum(jnp.where(at_rank, picked, 0.0), axis=0, keepdims=True)
    out_ref[...] = jnp.log(1.0 + total)


def body(embeddings, cluster_ids):
    count, width = embeddings.shape
    dma = pltpu.SemaphoreType.DMA
    vmem = pl.BlockSpec(memory_space=pltpu.VMEM)
    out = pl.pallas_call(
        kernel,
        out_shape=jax.ShapeDtypeStruct((1, count), jnp.float32),
        in_specs=[vmem, vmem],
        out_specs=vmem,
        scratch_shapes=[
            pltpu.VMEM((count, width), jnp.bfloat16),
            pltpu.VMEM((SHARDS, CAP, width), jnp.bfloat16),
            pltpu.VMEM((SHARDS, 1, LANES), jnp.float32),
            pltpu.VMEM((3, SLOTS, width), jnp.bfloat16),
            pltpu.VMEM((3, SHARDS, 1, LANES), jnp.float32),
            pltpu.VMEM((SLOTS, LANES), jnp.float32),
            pltpu.VMEM((SLOTS, LANES), jnp.float32),
            pltpu.VMEM((SLOTS // LANES, 1, LANES), jnp.float32),
            pltpu.VMEM((SLOTS // LANES, 1, LANES), jnp.float32),
            pltpu.VMEM((2, SLOTS // LANES, 1, LANES), jnp.float32),
            pltpu.VMEM((SLOTS // LANES, 1, LANES), jnp.float32),
            pltpu.VMEM((SHARDS, 1, LANES), jnp.float32),
            dma((2,)), dma((SHARDS,)), dma((SHARDS,)), dma((SHARDS,)), dma((SHARDS,)),
            dma((2, SHARDS)), dma((2, SHARDS)), dma((2,)), dma((2,)), dma((2,)), dma((2,)),
            dma((SHARDS,)), dma((SHARDS,)),
        ],
        compiler_params=pltpu.CompilerParams(collective_id=0, has_side_effects=True),
    )(embeddings, cluster_ids.reshape(1, count))
    return out.reshape(count)


def solution(mesh):
    in_specs = (P(("shard", "tile"), None), P(("shard", "tile")))
    out_specs = P(("shard", "tile"))
    return jax.shard_map(body, mesh=mesh, in_specs=in_specs, out_specs=out_specs, check_vma=False)
```
